32 devices in a mesh: slide: 2 (over x), row: 16 (over z, y, core).
Axes of the slice: x: 2, y: 2, z: 4, core: 2. Of those that a mesh axis runs over, the one named last changes fastest.
Arguments:
- query_states: bfloat16 [32, 1, 4, 64, 768], P(('slide', 'row')), parts along dimension 0, may hold values from -240 to 240
- key_states: bfloat16 [32, 1, 4, 64, 768], P(('slide', 'row')), parts along dimension 0, may hold values from -6 to 6
- value_states: bfloat16 [32, 1, 4, 64, 768], P(('slide', 'row')), parts along dimension 0, may hold values from -6 to 6
- grad_output: bfloat16 [32, 1, 4, 64, 768], P(('slide', 'row')), parts along dimension 0, may hold values from -6 to 6
- tissue_map: int32 [4, 32], P('slide'), parts along dimension 0, may hold values from 0 to 1, as said below
Outputs:
- attended: bfloat16 [32, 1, 4, 64, 768], P(('slide', 'row')), parts along dimension 0
- grad_query: bfloat16 [32, 1, 4, 64, 768], P(('slide', 'row')), parts along dimension 0
- grad_key: bfloat16 [32, 1, 4, 64, 768], P(('slide', 'row')), parts along dimension 0
- grad_value: bfloat16 [32, 1, 4, 64, 768], P(('slide', 'row')), parts along dimension 0
The draws below stay inside these ranges and needn't reach their ends.
There are 2 independent parts, one for each index of `slide`. The reference program is written for one: setup_inputs(seed, part) draws one part's arguments, and reference() takes and returns one part's arrays. A program takes and returns all parts, laid end to end along the dimension named above; each array names one. Nothing has to cross between parts.
Inputs may be any that keep to these rules, and one draw needn't show every extreme that they name: `tissue_map`: 1 marks a tile that holds tissue; every tile of tile row 1 holds tissue.
All inputs are finite; a program needn't handle non-finite values.
Results may differ from the reference program's by a relative error of at most 0.023.
Values may be sent and summed in bfloat16 or wider, within the bound.
A program may use at most 128 MiB of HBM per device.

```python
import jax
import jax.numpy as jnp
from jax import lax

HEADS = 12
HEAD_DIM = 64
TILE_SIDE = 8
WINDOW = 13
GRID_C = 8
TILE_ROWS = 1
TILE_COLS = 4
BLOCKS = 16
ROWS_ALL = 2
COLS_ALL = 32
PIXELS = 64
INNER = 768


def paired_keys(key):
    full_shape = (BLOCKS, TILE_ROWS, TILE_COLS, TILE_SIDE * TILE_SIDE, HEADS * HEAD_DIM)
    drawn_keys = jnp.clip(jax.random.normal(jax.random.fold_in(key, 11), full_shape, jnp.float32), -6.0, 6.0)
    return drawn_keys


def draw_key_states(key, part):
    drawn_keys = paired_keys(key)
    return drawn_keys.astype(jnp.bfloat16)


def draw_query_states(key, part):
    drawn_keys = paired_keys(key)
    full_shape = drawn_keys.shape
    queries = jnp.clip(jax.random.normal(jax.random.fold_in(key, 13), full_shape, jnp.float32), -6.0, 6.0)
    return queries.astype(jnp.bfloat16)


def draw_tissue_map(key, part):
    density = jax.random.randint(jax.random.fold_in(key, 21), (ROWS_ALL, 1), 10, 101)
    chance = jax.random.randint(jax.random.fold_in(key, 22), (ROWS_ALL, COLS_ALL), 0, 100)
    band = jnp.arange(ROWS_ALL, dtype=jnp.int32)[:, None] == ROWS_ALL // 2
    return ((chance < density) | band).astype(jnp.int32)


def block_levels(key, shape, split, low, high):
    level, own = 1.0, jax.random.fold_in(key, 6)
    for position, blocks in split:
        steps = jnp.exp(jax.random.uniform(jax.random.fold_in(own, position), (blocks,), jnp.float32, low / len(split), high / len(split)))
        level = level * jnp.repeat(steps, shape[position] // blocks).reshape([-1 if axis == position else 1 for axis in range(len(shape))])
    return level


def noise(own_key, extent, spread, bound, cuts=(), kind=jnp.bfloat16):
    loudness = block_levels(own_key, extent, cuts, -0.22, 0.18) if cuts else 1.0
    array = jax.random.normal(own_key, extent, jnp.float32) * spread * loudness
    return jnp.minimum(jnp.maximum(array, -bound), bound).astype(kind)


def setup_inputs(seed: int = 0, part: int = 0) -> dict:
    key_of = jax.random.split(jax.random.key(seed), 6)
    own_keys = jax.random.split(jax.random.fold_in(key_of[5], part), 6)
    query_states = draw_query_states(jax.random.fold_in(jax.random.fold_in(key_of[5], part), 71), part)
    key_states = draw_key_states(jax.random.fold_in(jax.random.fold_in(key_of[5], part), 71), part)
    value_states = noise(own_keys[2], (BLOCKS, TILE_ROWS, TILE_COLS, PIXELS, INNER), 1.0, 6.0, ((0, 16),))
    grad_output = noise(own_keys[3], (BLOCKS, TILE_ROWS, TILE_COLS, PIXELS, INNER), 1.0, 6.0, ((0, 16),))
    tissue_map = draw_tissue_map(jax.random.fold_in(jax.random.fold_in(key_of[5], part), 71), part)
    return dict(query_states=query_states, key_states=key_states, value_states=value_states, grad_output=grad_output, tissue_map=tissue_map)


MASKED_SCORE = -1e30


def window_table():
    half_window = (WINDOW - 1) // 2
    pixel_index = jnp.arange(TILE_SIDE * TILE_SIDE, dtype=jnp.int32)
    pix_row = pixel_index // TILE_SIDE
    pix_col = pixel_index % TILE_SIDE
    tables = []
    for row_step in (-1, 0, 1):
        for col_step in (-1, 0, 1):
            row_gap = TILE_SIDE * row_step + pix_row[None, :] - pix_row[:, None]
            col_gap = TILE_SIDE * col_step + pix_col[None, :] - pix_col[:, None]
            tables.append((jnp.abs(row_gap) <= half_window) & (jnp.abs(col_gap) <= half_window))
    return jnp.stack(tables)


def widen_to(operand, widen):
    if widen:
        return operand.astype(jnp.float32)
    return operand


def to_grid(operand):
    operand = jnp.roll(operand, GRID_C // 2, axis=0)
    block_count, tile_rows, tile_cols, pixel_count, inner_width = operand.shape
    grid_rows = block_count // GRID_C
    moved = operand.reshape(grid_rows, GRID_C, tile_rows, tile_cols, pixel_count, inner_width).transpose(0, 2, 1, 3, 4, 5)
    return moved.reshape(grid_rows * tile_rows, GRID_C * tile_cols, pixel_count, inner_width)


def to_blocks(operand):
    rows_all, cols_all, pixel_count, inner_width = operand.shape
    moved = operand.reshape(rows_all // TILE_ROWS, TILE_ROWS, GRID_C, TILE_COLS, pixel_count, inner_width).transpose(0, 2, 1, 3, 4, 5)
    moved = moved.reshape(-1, TILE_ROWS, TILE_COLS, pixel_count, inner_width)
    return jnp.roll(moved, -(GRID_C // 2), axis=0)


def attend_tiles(query4, grad4, key4, value4, allowed, tissue_rows, widen):
    score_scale = HEAD_DIM ** -0.5
    usable = allowed[:, None]
    scores = jnp.einsum("cqhe,ckhe->chqk", widen_to(query4, widen), widen_to(key4, widen), preferred_element_type=jnp.float32) * score_scale
    masked = jnp.where(usable, scores, MASKED_SCORE)
    row_peak = jnp.max(masked, axis=-1, keepdims=True)
    row_total = jnp.sum(jnp.exp(masked - row_peak), axis=-1, keepdims=True)
    log_total = row_peak + jnp.log(row_total)
    weights_full = jnp.where(usable, jnp.exp(scores - log_total), 0.0)
    weights_low = weights_full.astype(jnp.bfloat16)
    mixture = jnp.einsum("chqk,ckhe->cqhe", widen_to(weights_low, widen), widen_to(value4, widen), preferred_element_type=jnp.float32)
    attended = (mixture * tissue_rows[:, None, None, None]).astype(jnp.bfloat16)
    out_dot = jnp.einsum("cqhe,cqhe->chq", widen_to(attended, widen), widen_to(grad4, widen), preferred_element_type=jnp.float32)
    grad_probe = jnp.einsum("cqhe,ckhe->chqk", widen_to(grad4, widen), widen_to(value4, widen), preferred_element_type=jnp.float32)
    grad_score = (weights_full * (grad_probe - out_dot[..., None])).astype(jnp.bfloat16)
    grad_query = (jnp.einsum("chqk,ckhe->cqhe", widen_to(grad_score, widen), widen_to(key4, widen), preferred_element_type=jnp.float32) * score_scale).astype(jnp.bfloat16)
    grad_key = jnp.einsum("chqk,cqhe->ckhe", widen_to(grad_score, widen), widen_to(query4, widen), preferred_element_type=jnp.float32) * score_scale
    grad_value = jnp.einsum("chqk,cqhe->ckhe", widen_to(weights_low, widen), widen_to(grad4, widen), preferred_element_type=jnp.float32)
    return attended, grad_query, log_total[..., 0], out_dot, grad_key, grad_value


def key_terms(query4, grad4, key4, value4, allowed, log_total, out_dot, widen):
    score_scale = HEAD_DIM ** -0.5
    usable = allowed[:, None]
    scores = jnp.einsum("cqhe,ckhe->chqk", widen_to(query4, widen), widen_to(key4, widen), preferred_element_type=jnp.float32) * score_scale
    weights_full = jnp.where(usable, jnp.exp(scores - log_total[..., None]), 0.0)
    weights_low = weights_full.astype(jnp.bfloat16)
    grad_probe = jnp.einsum("cqhe,ckhe->chqk", widen_to(grad4, widen), widen_to(value4, widen), preferred_element_type=jnp.float32)
    grad_score = (weights_full * (grad_probe - out_dot[..., None])).astype(jnp.bfloat16)
    grad_key = jnp.einsum("chqk,cqhe->ckhe", widen_to(grad_score, widen), widen_to(query4, widen), preferred_element_type=jnp.float32) * score_scale
    grad_value = jnp.einsum("chqk,cqhe->ckhe", widen_to(weights_low, widen), widen_to(grad4, widen), preferred_element_type=jnp.float32)
    return grad_key, grad_value


def reference(query_states, key_states, value_states, grad_output, tissue_map):
    query_states = to_grid(query_states)
    key_states = to_grid(key_states)
    value_states = to_grid(value_states)
    grad_output = to_grid(grad_output)
    rows_all, column_total = tissue_map.shape
    pixel_count = TILE_SIDE * TILE_SIDE
    window_masks = window_table()
    tissue = tissue_map.astype(jnp.float32)
    grad_eff = (grad_output * tissue[:, :, None, None]).astype(jnp.bfloat16)

    def framed(operand):
        return jnp.pad(operand, ((1, 1), (1, 1), (0, 0), (0, 0)))

    key_pad = framed(key_states)
    value_pad = framed(value_states)
    tissue_pad = jnp.pad(tissue_map, ((1, 1), (1, 1)))

    def query_row(row_index):
        key_tiles, value_tiles, flag_tiles = [], [], []
        for row_step in (-1, 0, 1):
            where_row = row_index + 1 + row_step
            key_band = lax.dynamic_index_in_dim(key_pad, where_row, 0, keepdims=False)
            value_strip = lax.dynamic_index_in_dim(value_pad, where_row, 0, keepdims=False)
            flag_band = lax.dynamic_index_in_dim(tissue_pad, where_row, 0, keepdims=False)
            for col_step in (-1, 0, 1):
                key_tiles.append(key_band[1 + col_step:1 + col_step + column_total])
                value_tiles.append(value_strip[1 + col_step:1 + col_step + column_total])
                flag_tiles.append(flag_band[1 + col_step:1 + col_step + column_total])
        key4 = jnp.stack(key_tiles, 1).reshape(column_total, 9 * pixel_count, HEADS, HEAD_DIM)
        value4 = jnp.stack(value_tiles, 1).reshape(column_total, 9 * pixel_count, HEADS, HEAD_DIM)
        flags = jnp.stack(flag_tiles, 1)
        allowed = (window_masks.transpose(1, 0, 2)[None] & (flags[:, None, :, None] > 0)).reshape(column_total, pixel_count, 9 * pixel_count)
        query4 = lax.dynamic_index_in_dim(query_states, row_index, 0, keepdims=False).reshape(column_total, pixel_count, HEADS, HEAD_DIM)
        grad4 = lax.dynamic_index_in_dim(grad_eff, row_index, 0, keepdims=False).reshape(column_total, pixel_count, HEADS, HEAD_DIM)
        tissue_rows = lax.dynamic_index_in_dim(tissue, row_index, 0, keepdims=False)
        attended, grad_query, log_total, out_dot, unused_key, unused_value = attend_tiles(query4, grad4, key4, value4, allowed, tissue_rows, True)
        return attended.reshape(column_total, pixel_count, INNER), grad_query.reshape(column_total, pixel_count, INNER), log_total, out_dot

    row_ids = jnp.arange(rows_all, dtype=jnp.int32)
    attended, grad_query, log_total, out_dot = lax.map(query_row, row_ids)

    query_pad = framed(query_states)
    gradient_padded = framed(grad_eff)
    log_pad = framed(log_total)
    dot_pad = framed(out_dot)

    def key_row(row_index):
        query_tiles, grad_tiles, log_tiles, dot_tiles = [], [], [], []
        for row_step in (-1, 0, 1):
            where_row = row_index + 1 - row_step
            query_band = lax.dynamic_index_in_dim(query_pad, where_row, 0, keepdims=False)
            grad_band = lax.dynamic_index_in_dim(gradient_padded, where_row, 0, keepdims=False)
            log_band = lax.dynamic_index_in_dim(log_pad, where_row, 0, keepdims=False)
            dot_band = lax.dynamic_index_in_dim(dot_pad, where_row, 0, keepdims=False)
            for col_step in (-1, 0, 1):
                query_tiles.append(query_band[1 - col_step:1 - col_step + column_total])
                grad_tiles.append(grad_band[1 - col_step:1 - col_step + column_total])
                log_tiles.append(log_band[1 - col_step:1 - col_step + column_total])
                dot_tiles.append(dot_band[1 - col_step:1 - col_step + column_total])
        query4 = jnp.stack(query_tiles, 1).reshape(column_total, 9 * pixel_count, HEADS, HEAD_DIM)
        grad4 = jnp.stack(grad_tiles, 1).reshape(column_total, 9 * pixel_count, HEADS, HEAD_DIM)
        log4 = jnp.stack(log_tiles, 2).reshape(column_total, HEADS, 9 * pixel_count)
        dot4 = jnp.stack(dot_tiles, 2).reshape(column_total, HEADS, 9 * pixel_count)
        key4 = lax.dynamic_index_in_dim(key_states, row_index, 0, keepdims=False).reshape(column_total, pixel_count, HEADS, HEAD_DIM)
        value4 = lax.dynamic_index_in_dim(value_states, row_index, 0, keepdims=False).reshape(column_total, pixel_count, HEADS, HEAD_DIM)
        flags = lax.dynamic_index_in_dim(tissue_map, row_index, 0, keepdims=False)
        allowed = (window_masks[None] & (flags[:, None, None, None] > 0)).reshape(column_total, 9 * pixel_count, pixel_count)
        grad_key, grad_value = key_terms(query4, grad4, key4, value4, allowed, log4, dot4, True)
        return grad_key.astype(jnp.bfloat16).reshape(column_total, pixel_count, INNER), grad_value.astype(jnp.bfloat16).reshape(column_total, pixel_count, INNER)

    grad_key, grad_value = lax.map(key_row, row_ids)
    return (to_blocks(attended), to_blocks(grad_query), to_blocks(grad_key), to_blocks(grad_value))
```

```python
import functools

import jax
import jax.numpy as jnp
from jax import lax
from jax.experimental import pallas as pl
from jax.experimental.pallas import tpu as pltpu
from jax.sharding import PartitionSpec as P

HEAD_DIM = 64
TILE_SIDE = 8
WINDOW = 13
GRID_C = 8
PIX = TILE_SIDE * TILE_SIDE
HALF = (WINDOW - 1) // 2
REACH = HALF * TILE_SIDE
SKIP = PIX - REACH
WIDTH = 256
SUB = WIDTH // HEAD_DIM
MASKED = -1e30
F32 = jnp.float32
BF16 = jnp.bfloat16


def dot(a, b, ca, cb):
    return lax.dot_general(a, b, (((ca,), (cb,)), ((), ())), preferred_element_type=F32)


def fold_rows(x):
    total = x[:PIX]
    for i in range(1, SUB):
        total = total + x[i * PIX : (i + 1) * PIX]
    return total


def attend_kernel(nv, cols, flag_ref, q_ref, k_ref, v_ref, g_ref, bias_ref, left_ref, right_ref, *rest):
    vert = rest[:nv]
    rest = rest[nv:]
    rest = rest[-(5 + nv + 4) :]
    att_ref, dq_ref, own_ref, dleft_ref, dright_ref = rest[:5]
    dvert = rest[5 : 5 + nv]
    kx, vx, dkx, dvx = rest[5 + nv :]
    base = (cols + 2) * PIX
    span = (cols + 2) * REACH

    for z, (x, own) in enumerate(((kx, k_ref), (vx, v_ref))):
        x[0:PIX] = left_ref[z, 0:PIX]
        x[PIX : PIX * (cols + 1)] = own[...].reshape(cols * PIX, WIDTH)
        x[PIX * (cols + 1) : base] = right_ref[z, 0:PIX]
        for i in range(nv):
            at = base + i * span
            edge = PIX + i * REACH
            x[at : at + REACH] = left_ref[z, edge : edge + REACH]
            x[at + REACH : at + REACH * (cols + 1)] = vert[i][z].reshape(cols * REACH, WIDTH)
            x[at + REACH * (cols + 1) : at + span] = right_ref[z, edge : edge + REACH]
    dkx[...] = jnp.zeros_like(dkx)
    dvx[...] = jnp.zeros_like(dvx)

    same = (
        lax.broadcasted_iota(jnp.int32, (WIDTH, WIDTH), 0) // PIX
        == lax.broadcasted_iota(jnp.int32, (WIDTH, WIDTH), 1) // HEAD_DIM
    )
    same_low = jnp.where(same, 1.0, 0.0).astype(BF16)

    for c in range(cols):
        flag = flag_ref[c].astype(F32)
        live = jnp.where(same, flag, 0.0)
        q = q_ref[c] * 0.125
        qbd = jnp.concatenate([q] * SUB, axis=0) * same_low
        g = g_ref[c]
        gbd = jnp.concatenate([g] * SUB, axis=0) * live.astype(BF16)
        spans = [(c * PIX, 3 * PIX)] + [(base + i * span + c * REACH, 3 * REACH) for i in range(nv)]
        kc = jnp.concatenate([kx[at : at + n] for at, n in spans], axis=0)
        vc = jnp.concatenate([vx[at : at + n] for at, n in spans], axis=0)
        s = dot(kc, qbd, 1, 1) + bias_ref[c]
        peak = jnp.max(s, axis=0, keepdims=True)
        p = jnp.exp(s - peak)
        w = p * (1.0 / jnp.sum(p, axis=0, keepdims=True))
        w_low = w.astype(BF16)
        att_t = (dot(vc, w_low, 0, 0) * live).astype(BF16)
        att_ref[c] = fold_rows(att_t.T)
        out_dot = jnp.sum(att_t.astype(F32) * gbd.T.astype(F32), axis=0, keepdims=True)
        probe = dot(vc, gbd, 1, 1)
        ds = (w * (probe - out_dot)).astype(BF16)
        dq = jnp.where(same, dot(ds, kc, 0, 0), 0.0)
        dq_ref[c] = (fold_rows(dq) * 0.125).astype(BF16)
        dk = dot(ds, qbd, 1, 0)
        dv = dot(w_low, gbd, 1, 0)
        row = 0
        for at, n in spans:
            dkx[at : at + n] += dk[row : row + n]
            dvx[at : at + n] += dv[row : row + n]
            row += n

    for z, x in enumerate((dkx, dvx)):
        dleft_ref[z, 0:PIX] = x[0:PIX].astype(BF16)
        own_ref[z] = x[PIX : PIX * (cols + 1)].reshape(cols, PIX, WIDTH)
        dright_ref[z, 0:PIX] = x[PIX * (cols + 1) : base].astype(BF16)
        for i in range(nv):
            at = base + i * span
            edge = PIX + i * REACH
            dleft_ref[z, edge : edge + REACH] = x[at : at + REACH].astype(BF16)
            dvert[i][z] = x[at + REACH : at + REACH * (cols + 1)].reshape(cols, REACH, WIDTH)
            dright_ref[z, edge : edge + REACH] = x[at + REACH * (cols + 1) : at + span].astype(BF16)


def attend(group, flags, q, k, v, g, bias, left, right, vert, carried):
    cols, _, inner = q.shape
    nv = len(vert)
    keys = (cols + 2) * (PIX + nv * REACH)
    side = PIX + nv * REACH
    column = pl.BlockSpec((cols, PIX, WIDTH), lambda i: (0, 0, group))

    def full(x):
        return pl.BlockSpec(x.shape, lambda i: (0,) * len(x.shape))

    operands = [flags, q, k, v, g, bias, left, right, *vert]
    in_specs = [pl.BlockSpec(memory_space=pltpu.SMEM), column, column, column, column]
    in_specs += [full(x) for x in operands[5:]]
    aliases = {}
    if carried is not None:
        for j, x in enumerate(carried):
            aliases[len(operands)] = j
            operands.append(x)
            in_specs.append(pl.BlockSpec(memory_space=pl.ANY))
    out_shape = [jax.ShapeDtypeStruct(q.shape, BF16)] * 2
    out_shape += [jax.ShapeDtypeStruct((2, cols, PIX, WIDTH), F32)]
    out_shape += [jax.ShapeDtypeStruct((2, side, WIDTH), BF16)] * 2
    out_shape += [jax.ShapeDtypeStruct((2, cols, REACH, WIDTH), F32)] * nv
    seen = cols * 3 * (PIX + nv * REACH)
    return pl.pallas_call(
        functools.partial(attend_kernel, nv, cols),
        grid=(1,),
        in_specs=in_specs,
        out_specs=[column, column] + [full(x) for x in out_shape[2:]],
        out_shape=out_shape,
        scratch_shapes=[
            pltpu.VMEM((keys, WIDTH), BF16),
            pltpu.VMEM((keys, WIDTH), BF16),
            pltpu.VMEM((keys, WIDTH), F32),
            pltpu.VMEM((keys, WIDTH), F32),
        ],
        input_output_aliases=aliases,
        compiler_params=pltpu.CompilerParams(vmem_limit_bytes=40 << 20),
        cost_estimate=pl.CostEstimate(
            flops=seen * WIDTH * WIDTH * 2 * 6,
            bytes_accessed=8 << 20,
            transcendentals=seen * WIDTH,
        ),
    )(*operands)


def merge_kernel(nv, cols, *refs):
    from_left, from_right = refs[:2]
    dvert = refs[2 : 2 + nv]
    outs = refs[2 + nv :]
    for i in range(nv):
        edge = PIX + i * REACH
        for z in range(2):
            for c in range(cols):
                x = dvert[i][z, c]
                if c == 0:
                    x = x + from_left[z, edge : edge + REACH].astype(F32)
                if c == cols - 1:
                    x = x + from_right[z, edge : edge + REACH].astype(F32)
                outs[i][z, c] = x.astype(BF16)


def merge(from_left, from_right, dvert):
    cols = dvert[0].shape[1]
    return pl.pallas_call(
        functools.partial(merge_kernel, len(dvert), cols),
        out_shape=[jax.ShapeDtypeStruct(x.shape, BF16) for x in dvert],
        cost_estimate=pl.CostEstimate(flops=1 << 20, bytes_accessed=4 << 20, transcendentals=0),
    )(from_left, from_right, *dvert)


def finish_kernel(nv, cols, start_ref, own_ref, left_ref, right_ref, *rest):
    vert = rest[:nv]
    outs = rest[-3:-1]
    total = rest[-1]
    for z in range(2):
        total[...] = own_ref[z]
        total[0] += left_ref[z, 0:PIX].astype(F32)
        total[cols - 1] += right_ref[z, 0:PIX].astype(F32)
        for i in range(nv):
            at = pl.multiple_of(start_ref[i], TILE_SIDE)
            total[:, pl.ds(at, REACH), :] += vert[i][z].astype(F32)
        outs[z][...] = total[...].astype(BF16)


def finish(group, starts, own, from_left, from_right, vert, shape, carried):
    cols = own.shape[1]
    nv = len(vert)

    def full(x):
        return pl.BlockSpec(x.shape, lambda i: (0,) * len(x.shape))

    column = pl.BlockSpec((cols, PIX, WIDTH), lambda i: (0, 0, group))
    operands = [starts, own, from_left, from_right, *vert]
    in_specs = [pl.BlockSpec(memory_space=pltpu.SMEM)] + [full(x) for x in operands[1:]]
    aliases = {}
    if carried is not None:
        for j, x in enumerate(carried):
            aliases[len(operands)] = j
            operands.append(x)
            in_specs.append(pl.BlockSpec(memory_space=pl.ANY))
    return pl.pallas_call(
        functools.partial(finish_kernel, nv, cols),
        grid=(1,),
        in_specs=in_specs,
        out_specs=[column, column],
        out_shape=[jax.ShapeDtypeStruct(shape, BF16)] * 2,
        scratch_shapes=[pltpu.VMEM((cols, PIX, WIDTH), F32)],
        input_output_aliases=aliases,
        cost_estimate=pl.CostEstimate(flops=1 << 20, bytes_accessed=4 << 20, transcendentals=0),
    )(*operands)


def passed(block, distance):
    n = lax.axis_size("row")
    return lax.ppermute(block, "row", [((i - distance) % n, i) for i in range(n)])


def bias_table(band, places, cols):
    query = jnp.arange(WIDTH, dtype=jnp.int32) % PIX
    parts = []
    for band_row, first, rows in places:
        line = jnp.arange(rows * TILE_SIDE, dtype=jnp.int32)
        row_gap = first + (line // TILE_SIDE)[:, None] - (query // TILE_SIDE)[None, :]
        flags = lax.dynamic_index_in_dim(band, band_row, 0, keepdims=False)
        for step in (-1, 0, 1):
            col_gap = TILE_SIDE * step + (line % TILE_SIDE)[:, None] - (query % TILE_SIDE)[None, :]
            near = (jnp.abs(row_gap) <= HALF) & (jnp.abs(col_gap) <= HALF)
            live = flags[1 + step : 1 + step + cols] > 0
            parts.append(jnp.where(near[None] & live[:, None, None], 0.0, MASKED))
    return jnp.concatenate(parts, axis=1)


def local(query_states, key_states, value_states, grad_output, tissue_map):
    shape = query_states.shape
    cols, inner = shape[2], shape[4]
    q, k, v, g = (x.reshape(cols, PIX, inner) for x in (query_states, key_states, value_states, grad_output))
    count = lax.axis_size("row")
    block_rows = count // GRID_C
    block = (lax.axis_index("row") + GRID_C // 2) % count
    grid_row = block // GRID_C
    grid_col = block % GRID_C
    band = lax.dynamic_slice(
        jnp.pad(tissue_map, ((1, 1), (1, 1))), (grid_row, grid_col * cols), (3, cols + 2)
    )
    key_rows = REACH // TILE_SIDE
    places = [(1, 0, TILE_SIDE)]
    if block_rows == 2:
        above = grid_row == 1
        places.append((jnp.where(above, 0, 2), jnp.where(above, -HALF, TILE_SIDE), key_rows))
        ways = [(GRID_C, jnp.where(above, 0, SKIP))]
    elif block_rows > 2:
        places += [(0, -HALF, key_rows), (2, TILE_SIDE, key_rows)]
        ways = [(GRID_C, SKIP), (-GRID_C, 0)]
    else:
        ways = []
    nv = len(ways)
    starts = jnp.stack([jnp.asarray(start, jnp.int32) for _, start in ways] or [jnp.int32(0)])
    bias = bias_table(band, places, cols)
    flags = band[1, 1 : cols + 1]

    groups = inner // WIDTH
    received = []
    for i in range(groups):
        part = slice(i * WIDTH, (i + 1) * WIDTH)
        kv = jnp.stack([k[:, :, part], v[:, :, part]])
        received.append((kv, [
            passed(lax.dynamic_slice_in_dim(kv, start, REACH, 2), distance) for distance, start in ways
        ]))
    ready = []
    for kv, vert in received:
        def edge(c):
            return jnp.concatenate([kv[:, c]] + [x[:, c] for x in vert], axis=1)
        ready.append((passed(edge(cols - 1), 1), passed(edge(0), -1), vert))

    carried = None
    pending = []
    for i, (left, right, vert) in enumerate(ready):
        out = attend(i, flags, q, k, v, g, bias, left, right, vert, carried)
        carried = out[:2]
        own, dleft, dright, *dvert = out[2:]
        from_right = passed(dleft, -1)
        from_left = passed(dright, 1)
        if nv:
            sent = merge(from_left, from_right, dvert)
            back = [passed(x, -distance) for x, (distance, _) in zip(sent, ways)]
        else:
            back = []
        pending.append((own, from_left, from_right, back))
    grads = None
    for i, (own, from_left, from_right, back) in enumerate(pending):
        grads = finish(i, starts, own, from_left, from_right, back, (cols, PIX, inner), grads)
    return tuple(x.reshape(shape) for x in (*carried, *grads))


def solution(mesh):
    blocks = P(("slide", "row"), None, None, None, None)
    return jax.shard_map(
        local,
        mesh=mesh,
        in_specs=(blocks, blocks, blocks, blocks, P("slide", None)),
        out_specs=(blocks, blocks, blocks, blocks),
        check_vma=False,
    )
```

```python
import functools

import jax
import jax.numpy as jnp
from jax import lax
from jax.experimental import pallas as pl
from jax.experimental.pallas import tpu as pltpu
from jax.sharding import PartitionSpec as P

HEAD_DIM = 64
TILE_SIDE = 8
WINDOW = 13
GRID_C = 8
PIX = TILE_SIDE * TILE_SIDE
HALF = (WINDOW - 1) // 2
REACH = HALF * TILE_SIDE
SKIP = PIX - REACH
WIDTH = 256
SUB = WIDTH // HEAD_DIM
MASKED = -1e30
F32 = jnp.float32
BF16 = jnp.bfloat16


def dot(a, b, ca, cb):
    return lax.dot_general(a, b, (((ca,), (cb,)), ((), ())), preferred_element_type=F32)


def fold_rows(x):
    total = x[:PIX]
    for i in range(1, SUB):
        total = total + x[i * PIX : (i + 1) * PIX]
    return total


def ways_of(count, me):
    block_rows = count // GRID_C
    block = lax.rem(me + GRID_C // 2, count)
    grid_row = lax.div(block, GRID_C)
    grid_col = lax.rem(block, GRID_C)
    below = lax.rem(me + GRID_C, count)
    above = lax.rem(me + count - GRID_C, count)
    if block_rows == 2:
        ways = [(below, below, (1 - grid_row) * SKIP, 1 - grid_row, TILE_SIDE - grid_row * (TILE_SIDE + HALF))]
    elif block_rows > 2:
        ways = [
            (below, above, SKIP, grid_row - 1, -HALF),
            (above, below, 0, grid_row + 1, TILE_SIDE),
        ]
    else:
        ways = []
    return grid_row, grid_col, ways


def kernel(
    count, nv, tissue_ref, q_ref, k_ref, v_ref, g_ref, att_ref, dq_ref, dk_ref, dv_ref,
    frame, vframe, bias, acc, vacc, side_out, side_in, vert_out, vert_in,
    edge_s, edge_r, vert_s, vert_r, corner_s, corner_r, sg_s, sg_r, vg_s, vg_r,
):
    cols, _, inner = q_ref.shape
    groups = inner // WIDTH
    me = lax.axis_index("row")
    right = lax.rem(me + 1, count)
    left = lax.rem(me + count - 1, count)
    grid_row, grid_col, ways = ways_of(count, me)

    def remote(src, dst, send, recv, device):
        return pltpu.make_async_remote_copy(
            src_ref=src, dst_ref=dst, send_sem=send, recv_sem=recv,
            device_id={"row": device}, device_id_type=pl.DeviceIdType.MESH,
        )

    barrier = pltpu.get_barrier_semaphore()
    for device in [left, right] + [way[0] for way in ways]:
        pl.semaphore_signal(
            barrier, inc=1, device_id={"row": device}, device_id_type=pl.DeviceIdType.MESH
        )
    pl.semaphore_wait(barrier, 2 + nv)

    inputs = (k_ref, v_ref)

    def part(g):
        return pl.ds(g * WIDTH, WIDTH)

    vertical = []
    for g in range(groups):
        copies = []
        for i, (to, _, start, _, _) in enumerate(ways):
            for z in range(2):
                copies.append(remote(
                    inputs[z].at[:, pl.ds(pl.multiple_of(start, 16), REACH), part(g)],
                    vframe.at[i, z, pl.ds(1, cols), :, part(g)],
                    vert_s.at[i, z, g], vert_r.at[i, z, g], to,
                ))
        vertical.append(copies)
    edges = []
    for z in range(2):
        edges.append(remote(inputs[z].at[cols - 1], frame.at[z, 0], edge_s.at[0, z], edge_r.at[0, z], right))
        edges.append(remote(inputs[z].at[0], frame.at[z, cols + 1], edge_s.at[1, z], edge_r.at[1, z], left))
    corners, side_grads, vert_grads = [], [], []
    for g in range(groups):
        copies = []
        for i in range(nv):
            copies.append(remote(
                vframe.at[i, :, cols, :, part(g)], vframe.at[i, :, 0, :, part(g)],
                corner_s.at[i, 0, g], corner_r.at[i, 0, g], right,
            ))
            copies.append(remote(
                vframe.at[i, :, 1, :, part(g)], vframe.at[i, :, cols + 1, :, part(g)],
                corner_s.at[i, 1, g], corner_r.at[i, 1, g], left,
            ))
        corners.append(copies)
        side_grads.append([
            remote(side_out.at[0, :, :, part(g)], side_in.at[1, :, :, part(g)], sg_s.at[0, g], sg_r.at[0, g], left),
            remote(side_out.at[1, :, :, part(g)], side_in.at[0, :, :, part(g)], sg_s.at[1, g], sg_r.at[1, g], right),
        ])
        vert_grads.append([
            remote(
                vert_out.at[i, :, :, :, part(g)], vert_in.at[i, :, :, :, part(g)],
                vg_s.at[i, g], vg_r.at[i, g], ways[i][1],
            )
            for i in range(nv)
        ])

    for copy in vertical[0] + edges:
        copy.start()

    for z in range(2):
        frame[z, 1 : cols + 1] = inputs[z][...]
    acc[...] = jnp.zeros_like(acc)
    if nv:
        vacc[...] = jnp.zeros_like(vacc)

    rows_all, cols_all = tissue_ref.shape

    def flag_at(row, col):
        inside = jnp.where((row >= 0) & (row < rows_all) & (col >= 0) & (col < cols_all), 1, 0)
        value = tissue_ref[jnp.clip(row, 0, rows_all - 1), jnp.clip(col, 0, cols_all - 1)]
        return (value * inside).astype(F32)

    at = 0
    for row, first, lines in [(grid_row, 0, PIX)] + [(way[3], way[4], REACH) for way in ways]:
        flags = [flag_at(row, grid_col * cols + col) for col in range(-1, cols + 1)]
        line = lax.broadcasted_iota(jnp.int32, (lines, WIDTH), 0)
        query = lax.broadcasted_iota(jnp.int32, (lines, WIDTH), 1) & (PIX - 1)
        row_gap = first + (line >> 3) - (query >> 3)
        for step in (-1, 0, 1):
            col_gap = TILE_SIDE * step + (line & 7) - (query & 7)
            near = (jnp.abs(row_gap) <= HALF) & (jnp.abs(col_gap) <= HALF)
            near = jnp.where(near, 0.0, MASKED)
            for c in range(cols):
                bias[c, at : at + lines] = near + (flags[c + 1 + step] - 1.0) * -MASKED
            at += lines

    same = (
        lax.broadcasted_iota(jnp.int32, (WIDTH, WIDTH), 0) // PIX
        == lax.broadcasted_iota(jnp.int32, (WIDTH, WIDTH), 1) // HEAD_DIM
    )
    same_f = jnp.where(same, 1.0, 0.0)

    def attend(g):
        columns = part(g)

        def body(c, _):
            live = same_f * flag_at(grid_row, grid_col * cols + c)
            q = q_ref[c, :, columns] * 0.125
            qbd = jnp.concatenate([q] * SUB, axis=0) * same_f.astype(BF16)
            grad = g_ref[c, :, columns]
            gbd = jnp.concatenate([grad] * SUB, axis=0) * live.astype(BF16)
            reach = pl.ds(c, 3)

            def keys(z):
                pieces = [frame[z, reach, :, columns].reshape(3 * PIX, WIDTH)]
                for i in range(nv):
                    pieces.append(vframe[i, z, reach, :, columns].reshape(3 * REACH, WIDTH))
                return jnp.concatenate(pieces, axis=0)

            kc, vc = keys(0), keys(1)
            s = dot(kc, qbd, 1, 1) + bias[c]
            peak = jnp.max(s, axis=0, keepdims=True)
            p = jnp.exp(s - peak)
            w = p * (1.0 / jnp.sum(p, axis=0, keepdims=True))
            w_low = w.astype(BF16)
            att_t = (dot(vc, w_low, 0, 0) * live).astype(BF16)
            att_ref[c, :, columns] = fold_rows(att_t.T)
            out_dot = jnp.sum(att_t.astype(F32) * gbd.T.astype(F32), axis=0, keepdims=True)
            probe = dot(vc, gbd, 1, 1)
            ds = (w * (probe - out_dot)).astype(BF16)
            dq = dot(ds, kc, 0, 0) * same_f
            dq_ref[c, :, columns] = (fold_rows(dq) * 0.125).astype(BF16)
            for z, d in enumerate((dot(ds, qbd, 1, 0), dot(w_low, gbd, 1, 0))):
                acc[z, reach, :, columns] += d[: 3 * PIX].reshape(3, PIX, WIDTH)
                for i in range(nv):
                    row = 3 * (PIX + i * REACH)
                    vacc[i, z, reach, :, columns] += d[row : row + 3 * REACH].reshape(3, REACH, WIDTH)
            return 0

        lax.fori_loop(0, cols, body, 0)
        for z in range(2):
            for side, tile in ((0, 0), (1, cols + 1)):
                side_out[side, z, 0:PIX, columns] = acc[z, tile, :, columns].astype(BF16)
                for i in range(nv):
                    edge = PIX + i * REACH
                    side_out[side, z, edge : edge + REACH, columns] = vacc[i, z, tile, :, columns].astype(BF16)
        for copy in side_grads[g]:
            copy.start()

    def arrive(g):
        for copy in vertical[g]:
            copy.wait()
        if g + 1 < groups:
            for copy in vertical[g + 1]:
                copy.start()
        for copy in corners[g]:
            copy.start()

    def give_back(g):
        columns = part(g)
        for copy in side_grads[g]:
            copy.wait()
        for z in range(2):
            for side, tile in ((0, 1), (1, cols)):
                acc[z, tile, :, columns] += side_in[side, z, 0:PIX, columns].astype(F32)
                for i in range(nv):
                    edge = PIX + i * REACH
                    vacc[i, z, tile, :, columns] += side_in[side, z, edge : edge + REACH, columns].astype(F32)
            for i in range(nv):
                vert_out[i, z, :, :, columns] = vacc[i, z, 1 : cols + 1, :, columns].astype(BF16)
        for copy in vert_grads[g]:
            copy.start()

    def finish(g):
        columns = part(g)
        for copy in vert_grads[g]:
            copy.wait()
        for z, out in enumerate((dk_ref, dv_ref)):
            for i in range(nv):
                lines = pl.ds(pl.multiple_of(ways[i][2], 16), REACH)
                acc[z, pl.ds(1, cols), lines, columns] += vert_in[i, z, :, :, columns].astype(F32)
            out[:, :, columns] = acc[z, 1 : cols + 1, :, columns].astype(BF16)

    arrive(0)
    for copy in edges:
        copy.wait()
    for g in range(groups):
        for copy in corners[g]:
            copy.wait()
        attend(g)
        if g + 1 < groups:
            arrive(g + 1)
        give_back(g)
    for g in range(groups):
        finish(g)


def local(query_states, key_states, value_states, grad_output, tissue_map):
    shape = query_states.shape
    cols, inner = shape[2], shape[4]
    q, k, v, g = (x.reshape(cols, PIX, inner) for x in (query_states, key_states, value_states, grad_output))
    count = lax.axis_size("row")
    nv = min(2, count // GRID_C - 1)
    groups = inner // WIDTH
    strips = max(nv, 1)
    side = PIX + nv * REACH
    dma = pltpu.SemaphoreType.DMA
    out = pl.pallas_call(
        functools.partial(kernel, count, nv),
        in_specs=[pl.BlockSpec(memory_space=pltpu.SMEM)] + [pl.BlockSpec(memory_space=pltpu.VMEM)] * 4,
        out_specs=[pl.BlockSpec(memory_space=pltpu.VMEM)] * 4,
        out_shape=[jax.ShapeDtypeStruct(q.shape, BF16)] * 4,
        scratch_shapes=[
            pltpu.VMEM((2, cols + 2, PIX, inner), BF16),
            pltpu.VMEM((strips, 2, cols + 2, REACH, inner), BF16),
            pltpu.VMEM((cols, 3 * side, WIDTH), F32),
            pltpu.VMEM((2, cols + 2, PIX, inner), F32),
            pltpu.VMEM((strips, 2, cols + 2, REACH, inner), F32),
            pltpu.VMEM((2, 2, side, inner), BF16),
            pltpu.VMEM((2, 2, side, inner), BF16),
            pltpu.VMEM((strips, 2, cols, REACH, inner), BF16),
            pltpu.VMEM((strips, 2, cols, REACH, inner), BF16),
            dma((2, 2)), dma((2, 2)),
            dma((strips, 2, groups)), dma((strips, 2, groups)),
            dma((strips, 2, groups)), dma((strips, 2, groups)),
            dma((2, groups)), dma((2, groups)),
            dma((strips, groups)), dma((strips, groups)),
        ],
        compiler_params=pltpu.CompilerParams(
            collective_id=0, has_side_effects=True, vmem_limit_bytes=48 << 20
        ),
    )(tissue_map, q, k, v, g)
    return tuple(x.reshape(shape) for x in out)


def solution(mesh):
    blocks = P(("slide", "row"), None, None, None, None)
    return jax.shard_map(
        local,
        mesh=mesh,
        in_specs=(blocks, blocks, blocks, blocks, P("slide", None)),
        out_specs=(blocks, blocks, blocks, blocks),
        check_vma=False,
    )
```

```python
import functools

import jax
import jax.numpy as jnp
from jax import lax
from jax.experimental import pallas as pl
from jax.experimental.pallas import tpu as pltpu
from jax.sharding import PartitionSpec as P

HEAD_DIM = 64
TILE_SIDE = 8
WINDOW = 13
GRID_C = 8
PIX = TILE_SIDE * TILE_SIDE
HALF = (WINDOW - 1) // 2
REACH = HALF * TILE_SIDE
SKIP = PIX - REACH
WIDTH = 256
SUB = WIDTH // HEAD_DIM
MASKED = -1e30
LEAD = 1
F32 = jnp.float32
BF16 = jnp.bfloat16


def dot(a, b, ca, cb):
    return lax.dot_general(a, b, (((ca,), (cb,)), ((), ())), preferred_element_type=F32)


def fold_rows(x):
    total = x[:PIX]
    for i in range(1, SUB):
        total = total + x[i * PIX : (i + 1) * PIX]
    return total


def ways_of(count, me):
    block_rows = count // GRID_C
    block = lax.rem(me + GRID_C // 2, count)
    grid_row = lax.div(block, GRID_C)
    grid_col = lax.rem(block, GRID_C)
    below = lax.rem(me + GRID_C, count)
    above = lax.rem(me + count - GRID_C, count)
    if block_rows == 2:
        ways = [(below, below, (1 - grid_row) * SKIP, 1 - grid_row, TILE_SIDE - grid_row * (TILE_SIDE + HALF))]
    elif block_rows > 2:
        ways = [
            (below, above, SKIP, grid_row - 1, -HALF),
            (above, below, 0, grid_row + 1, TILE_SIDE),
        ]
    else:
        ways = []
    return grid_row, grid_col, ways


def kernel(
    count, nv, tissue_hbm, q_hbm, k_hbm, v_hbm, g_hbm, att_ref, dq_ref, dk_ref, dv_ref,
    tissue, query, grad_out, stage, frame, vframe, bias, acc, vacc, side_out, side_in, vert_out, vert_in,
    small_sem, frame_sem, stage_sem,
    edge_s, edge_r, vert_s, vert_r, corner_s, corner_r, sg_s, sg_r, vg_s, vg_r,
):
    cols, _, inner = q_hbm.shape
    groups = inner // WIDTH
    me = lax.axis_index("row")
    right = lax.rem(me + 1, count)
    left = lax.rem(me + count - 1, count)
    grid_row, grid_col, ways = ways_of(count, me)

    def remote(src, dst, send, recv, device):
        return pltpu.make_async_remote_copy(
            src_ref=src, dst_ref=dst, send_sem=send, recv_sem=recv,
            device_id={"row": device}, device_id_type=pl.DeviceIdType.MESH,
        )

    def part(g):
        return pl.ds(g * WIDTH, WIDTH)

    inputs = (k_hbm, v_hbm)
    staging = [
        [
            pltpu.make_async_copy(
                inputs[z].at[:, pl.ds(pl.multiple_of(way[2], 16), REACH), part(g)],
                stage.at[g, i, :, z], stage_sem.at[g, i, z],
            )
            for i, way in enumerate(ways)
            for z in range(2)
        ]
        for g in range(groups)
    ]
    framing = [
        pltpu.make_async_copy(inputs[z], frame.at[pl.ds(1, cols), z], frame_sem.at[z]) for z in range(2)
    ]
    flag_copy = pltpu.make_async_copy(tissue_hbm, tissue, small_sem.at[0])
    own_copies = [
        pltpu.make_async_copy(q_hbm, query, small_sem.at[1]),
        pltpu.make_async_copy(g_hbm, grad_out, small_sem.at[2]),
    ]
    for copy in [*staging[0], *framing, flag_copy, *sum(staging[1:], []), *own_copies]:
        copy.start()

    barrier = pltpu.get_barrier_semaphore()
    for device in [left, right] + [way[0] for way in ways]:
        pl.semaphore_signal(
            barrier, inc=1, device_id={"row": device}, device_id_type=pl.DeviceIdType.MESH
        )
    pl.semaphore_wait(barrier, 2 + nv)

    edges = [
        remote(frame.at[cols], frame.at[0], edge_s.at[0], edge_r.at[0], right),
        remote(frame.at[1], frame.at[cols + 1], edge_s.at[1], edge_r.at[1], left),
    ]
    vertical, corners, side_grads, inner_grads, outer_grads = [], [], [], [], []
    for g in range(groups):
        vertical.append([
            remote(stage.at[g, i], vframe.at[g, i, pl.ds(1, cols)], vert_s.at[i, g], vert_r.at[i, g], way[0])
            for i, way in enumerate(ways)
        ])
        corners.append(sum([
            [
                remote(vframe.at[g, i, cols], vframe.at[g, i, 0], corner_s.at[i, 0, g], corner_r.at[i, 0, g], right),
                remote(vframe.at[g, i, 1], vframe.at[g, i, cols + 1], corner_s.at[i, 1, g], corner_r.at[i, 1, g], left),
            ]
            for i in range(nv)
        ], []))
        side_grads.append([
            remote(side_out.at[g, 0], side_in.at[g, 1], sg_s.at[0, g], sg_r.at[0, g], left),
            remote(side_out.at[g, 1], side_in.at[g, 0], sg_s.at[1, g], sg_r.at[1, g], right),
        ])
        pieces = [
            [
                remote(
                    vert_out.at[g, i, pl.ds(first, size)], vert_in.at[g, i, pl.ds(first, size)],
                    vg_s.at[i, j, g], vg_r.at[i, j, g], ways[i][1],
                )
                for j, (first, size) in enumerate(((1, cols - 2), (0, 1), (cols - 1, 1)))
            ]
            for i in range(nv)
        ]
        inner_grads.append([x[0] for x in pieces])
        outer_grads.append(sum([x[1:] for x in pieces], []))

    def send_vertical(g):
        for copy in staging[g]:
            copy.wait()
        for copy in vertical[g]:
            copy.start()

    for g in range(LEAD):
        send_vertical(g)
    for copy in framing:
        copy.wait()
    for copy in edges:
        copy.start()

    acc[...] = jnp.zeros_like(acc)
    if nv:
        vacc[...] = jnp.zeros_like(vacc)
    flag_copy.wait()

    rows_all, cols_all = tissue.shape

    def flag_at(row, col):
        inside = jnp.where((row >= 0) & (row < rows_all) & (col >= 0) & (col < cols_all), 1, 0)
        value = tissue[jnp.clip(row, 0, rows_all - 1), jnp.clip(col, 0, cols_all - 1)]
        return (value * inside).astype(F32)

    at = 0
    for row, first, lines in [(grid_row, 0, PIX)] + [(way[3], way[4], REACH) for way in ways]:
        flags = [flag_at(row, grid_col * cols + col) for col in range(-1, cols + 1)]
        line = lax.broadcasted_iota(jnp.int32, (lines, WIDTH), 0)
        pixel = lax.broadcasted_iota(jnp.int32, (lines, WIDTH), 1) & (PIX - 1)
        row_gap = first + (line >> 3) - (pixel >> 3)
        for step in (-1, 0, 1):
            col_gap = TILE_SIDE * step + (line & 7) - (pixel & 7)
            near = (jnp.abs(row_gap) <= HALF) & (jnp.abs(col_gap) <= HALF)
            near = jnp.where(near, 0.0, MASKED)
            for c in range(cols):
                bias[c, at : at + lines] = near + (flags[c + 1 + step] - 1.0) * -MASKED
            at += lines

    same = (
        lax.broadcasted_iota(jnp.int32, (WIDTH, WIDTH), 0) // PIX
        == lax.broadcasted_iota(jnp.int32, (WIDTH, WIDTH), 1) // HEAD_DIM
    )
    same_f = jnp.where(same, 1.0, 0.0)
    for copy in own_copies:
        copy.wait()

    def attend(g, c):
        columns = part(g)
        live = same_f * flag_at(grid_row, grid_col * cols + c)
        q = query[c, :, columns] * 0.125
        qbd = jnp.concatenate([q] * SUB, axis=0) * same_f.astype(BF16)
        grad = grad_out[c, :, columns]
        gbd = jnp.concatenate([grad] * SUB, axis=0) * live.astype(BF16)

        def keys(z):
            pieces = [frame[c + j, z, :, columns] for j in range(3)]
            for i in range(nv):
                pieces += [vframe[g, i, c + j, z] for j in range(3)]
            return jnp.concatenate(pieces, axis=0)

        kc, vc = keys(0), keys(1)
        s = dot(kc, qbd, 1, 1) + bias[c]
        peak = jnp.max(s, axis=0, keepdims=True)
        p = jnp.exp(s - peak)
        w = p * (1.0 / jnp.sum(p, axis=0, keepdims=True))
        w_low = w.astype(BF16)
        att_t = (dot(vc, w_low, 0, 0) * live).astype(BF16)
        att_ref[c, :, columns] = fold_rows(att_t.T)
        out_dot = jnp.sum(att_t.astype(F32) * gbd.T.astype(F32), axis=0, keepdims=True)
        probe = dot(vc, gbd, 1, 1)
        ds = (w * (probe - out_dot)).astype(BF16)
        dq = dot(ds, kc, 0, 0) * same_f
        dq_ref[c, :, columns] = (fold_rows(dq) * 0.125).astype(BF16)
        for z, d in enumerate((dot(ds, qbd, 1, 0), dot(w_low, gbd, 1, 0))):
            acc[z, c : c + 3, :, columns] += d[: 3 * PIX].reshape(3, PIX, WIDTH)
            for i in range(nv):
                row = 3 * (PIX + i * REACH)
                vacc[g, i, z, c : c + 3] += d[row : row + 3 * REACH].reshape(3, REACH, WIDTH)

    def arrive(g):
        for copy in vertical[g]:
            copy.wait()
        if g + LEAD < groups:
            send_vertical(g + LEAD)
        for copy in corners[g]:
            copy.start()

    def give_sides(g):
        columns = part(g)
        for z in range(2):
            for side, tile in ((0, 0), (1, cols + 1)):
                side_out[g, side, z, 0:PIX] = acc[z, tile, :, columns].astype(BF16)
                for i in range(nv):
                    edge = PIX + i * REACH
                    side_out[g, side, z, edge : edge + REACH] = vacc[g, i, z, tile].astype(BF16)
        for copy in side_grads[g]:
            copy.start()
        for i in range(nv):
            for z in range(2):
                vert_out[g, i, 1 : cols - 1, z] = vacc[g, i, z, 2:cols].astype(BF16)
        for copy in inner_grads[g]:
            copy.start()

    def give_back(g):
        columns = part(g)
        for copy in side_grads[g]:
            copy.wait()
        for z in range(2):
            for side, tile in ((0, 1), (1, cols)):
                acc[z, tile, :, columns] += side_in[g, side, z, 0:PIX].astype(F32)
                for i in range(nv):
                    edge = PIX + i * REACH
                    term = side_in[g, side, z, edge : edge + REACH].astype(F32)
                    vert_out[g, i, tile - 1, z] = (vacc[g, i, z, tile] + term).astype(BF16)
        for copy in outer_grads[g]:
            copy.start()

    def finish(g):
        columns = part(g)
        for copy in inner_grads[g] + outer_grads[g]:
            copy.wait()
        for z, out in enumerate((dk_ref, dv_ref)):
            for i in range(nv):
                lines = pl.ds(pl.multiple_of(ways[i][2], 16), REACH)
                acc[z, pl.ds(1, cols), lines, columns] += vert_in[g, i, :, z].astype(F32)
            out[:, :, columns] = acc[z, 1 : cols + 1, :, columns].astype(BF16)

    arrive(0)
    for g in range(groups):
        for c in range(1, cols - 1):
            attend(g, c)
        if g == 0:
            for copy in edges:
                copy.wait()
        for copy in corners[g]:
            copy.wait()
        attend(g, 0)
        attend(g, cols - 1)
        give_sides(g)
        if g + 1 < groups:
            arrive(g + 1)
        give_back(g)
    for g in range(groups):
        finish(g)


def store_kernel(*refs):
    half = len(refs) // 2
    for i in range(half):
        refs[half + i][...] = refs[i][...]


def local(query_states, key_states, value_states, grad_output, tissue_map):
    shape = query_states.shape
    cols, inner = shape[2], shape[4]
    q, k, v, g = (x.reshape(cols, PIX, inner) for x in (query_states, key_states, value_states, grad_output))
    count = lax.axis_size("row")
    nv = min(2, count // GRID_C - 1)
    groups = inner // WIDTH
    strips = max(nv, 1)
    side = PIX + nv * REACH
    dma = pltpu.SemaphoreType.DMA
    vmem = pl.BlockSpec(memory_space=pltpu.VMEM)
    hbm = pl.BlockSpec(memory_space=pltpu.HBM)
    blocks = [jax.ShapeDtypeStruct(q.shape, BF16)] * 4
    out = pl.pallas_call(
        functools.partial(kernel, count, nv),
        in_specs=[hbm] * 5,
        out_specs=[vmem] * 4,
        out_shape=blocks,
        scratch_shapes=[
            pltpu.SMEM(tissue_map.shape, jnp.int32),
            pltpu.VMEM(q.shape, BF16),
            pltpu.VMEM(q.shape, BF16),
            pltpu.VMEM((groups, strips, cols, 2, REACH, WIDTH), BF16),
            pltpu.VMEM((cols + 2, 2, PIX, inner), BF16),
            pltpu.VMEM((groups, strips, cols + 2, 2, REACH, WIDTH), BF16),
            pltpu.VMEM((cols, 3 * side, WIDTH), F32),
            pltpu.VMEM((2, cols + 2, PIX, inner), F32),
            pltpu.VMEM((groups, strips, 2, cols + 2, REACH, WIDTH), F32),
            pltpu.VMEM((groups, 2, 2, side, WIDTH), BF16),
            pltpu.VMEM((groups, 2, 2, side, WIDTH), BF16),
            pltpu.VMEM((groups, strips, cols, 2, REACH, WIDTH), BF16),
            pltpu.VMEM((groups, strips, cols, 2, REACH, WIDTH), BF16),
            dma((3,)), dma((2,)), dma((groups, strips, 2)),
            dma((2,)), dma((2,)),
            dma((strips, groups)), dma((strips, groups)),
            dma((strips, 2, groups)), dma((strips, 2, groups)),
            dma((2, groups)), dma((2, groups)),
            dma((strips, 3, groups)), dma((strips, 3, groups)),
        ],
        compiler_params=pltpu.CompilerParams(
            collective_id=0, has_side_effects=True, vmem_limit_bytes=60 << 20
        ),
    )(tissue_map, q, k, v, g)
    tiles = pl.BlockSpec((1, PIX, inner), lambda i: (i, 0, 0))
    out = pl.pallas_call(
        store_kernel,
        grid=(cols,),
        in_specs=[tiles] * 4,
        out_specs=[tiles] * 4,
        out_shape=blocks,
        compiler_params=pltpu.CompilerParams(vmem_limit_bytes=60 << 20),
    )(*out)
    return tuple(x.reshape(shape) for x in out)


def solution(mesh):
    blocks = P(("slide", "row"), None, None, None, None)
    return jax.shard_map(
        local,
        mesh=mesh,
        in_specs=(blocks, blocks, blocks, blocks, P("slide", None)),
        out_specs=(blocks, blocks, blocks, blocks),
        check_vma=False,
    )
```
